128 devices in a mesh: blk: 64 (over y, z, x_hi, core), grp: 2 (over x_lo).
Axes of the slice: x: 4 (x_hi: 2, x_lo: 2; x = x_hi * 2 + x_lo), y: 4, z: 4, core: 2. Of those that a mesh axis runs over, the one named last changes fastest.
Arguments:
- x_pos: float32 [8, 98304], P(None, ('blk', 'grp')), may hold values from -6 to 6, as said below
- y_pos: float32 [8, 98304], P(None, ('blk', 'grp')), may hold values from -6 to 6, as said below
- f_pot: float32 [98304], P(('blk', 'grp')), may hold values from -8 to 260
- g_pot: float32 [98304], P(('blk', 'grp')), may hold values from -8 to 260
- x_logw: float32 [98304], P(('blk', 'grp')), may hold values from -1.5 to 1.5
- y_logw: float32 [98304], P(('blk', 'grp')), may hold values from -1.5 to 1.5
Outputs:
- f_out: float32 [98304], P(('blk', 'grp'))
- g_out: float32 [98304], P(('blk', 'grp'))
The draws below stay inside these ranges and needn't reach their ends.
Inputs may be any that keep to these rules, and one draw needn't show every extreme that they name: `x_pos`: states of both clouds. `y_pos`: states of both clouds.
All inputs are finite; a program needn't handle non-finite values.
Results may differ from the reference program's by a relative error of at most 0.0003.
Values sent between devices are 32-bit elements; how exact they have to be, the bound alone decides.
A program may use at most 64 MiB of HBM per device.

```python
import jax
import jax.numpy as jnp
from jax import lax

DIM = 8
PT_DEV = 768
STEPS = 8
NPTS = 98304
N_BLK = 64
N_GRP = 2


def draw_x_pos(key, part):
    key = jax.random.fold_in(key, 101)
    return jnp.clip(jax.random.normal(key, (DIM, NPTS), jnp.float32), -6.0, 6.0)


def draw_y_pos(key, part):
    key = jax.random.fold_in(key, 202)
    return jnp.clip(jax.random.normal(key, (DIM, NPTS), jnp.float32), -6.0, 6.0)


def draw_f_pot(key, part):
    key = jax.random.fold_in(key, 303)
    return jnp.clip(2.0 * jax.random.normal(key, (NPTS,), jnp.float32), -8.0, 8.0)


def draw_g_pot(key, part):
    key = jax.random.fold_in(key, 404)
    return jnp.clip(2.0 * jax.random.normal(key, (NPTS,), jnp.float32), -8.0, 8.0)


def shard_levels(rng, extent, cuts, low, largest):
    gain = 1.0
    for position, parts in cuts:
        draws = jax.random.uniform(jax.random.fold_in(jax.random.fold_in(rng, 6), position), (parts,), jnp.float32, low / len(cuts), largest / len(cuts))
        gain = gain * jnp.repeat(jnp.exp(draws), extent[position] // parts).reshape((-1,) + (1,) * (len(extent) - 1 - position))
    return gain


def setup_inputs(seed: int = 0) -> dict:
    keys = jax.random.split(jax.random.key(seed), 7)
    return {
        "x_pos": draw_x_pos(jax.random.fold_in(keys[6], 71), 0),
        "y_pos": draw_y_pos(jax.random.fold_in(keys[6], 71), 0),
        "f_pot": draw_f_pot(jax.random.fold_in(keys[6], 71), 0),
        "g_pot": draw_g_pot(jax.random.fold_in(keys[6], 71), 0),
        "x_logw": jnp.clip(jax.random.uniform(keys[4], (NPTS,), jnp.float32, -1.5, 1.5) * shard_levels(keys[4], (NPTS,), ((0, 128),), -0.4, 0.0), -1.5, 1.5),
        "y_logw": jnp.clip(jax.random.uniform(keys[5], (NPTS,), jnp.float32, -1.5, 1.5) * shard_levels(keys[5], (NPTS,), ((0, 128),), -0.4, 0.0), -1.5, 1.5),
    }


epsilon = 1.0
lowest = -1e30


def combine(first_max, first_sum, second_max, second_sum):
    top = jnp.maximum(first_max, second_max)
    return top, first_sum * jnp.exp(first_max - top) + second_sum * jnp.exp(second_max - top)


def piece_rows(rows):
    for candidate in (1024, 896, 768, 640, 512):
        if rows % candidate == 0:
            return candidate
    return rows


def tile_terms(sources, targets):
    source_pos, source_pot, source_logw = sources
    target_pos, target_pot, target_logw = targets
    rows = source_pot.shape[0]
    width = target_pot.shape[0]
    block_rows = piece_rows(rows)
    count = rows // block_rows
    target_half = 0.5 * jnp.sum(target_pos * target_pos, axis=0)
    target_term = target_logw + target_pot / epsilon

    def one_piece(carry, piece):
        column_max, column_sum = carry
        piece_pos, piece_pot, piece_logw = piece
        cross = lax.dot_general(piece_pos, target_pos, (((0,), (0,)), ((), ())), precision=lax.Precision.HIGHEST, preferred_element_type=jnp.float32)
        scaled = (0.5 * jnp.sum(piece_pos * piece_pos, axis=0)[:, None] + target_half[None, :] - cross) / epsilon
        row_score = target_term[None, :] - scaled
        row_max = jnp.max(row_score, axis=1)
        row_sum = jnp.sum(jnp.exp(row_score - row_max[:, None]), axis=1)
        column_score = (piece_logw + piece_pot / epsilon)[:, None] - scaled
        piece_max = jnp.max(column_score, axis=0)
        piece_sum = jnp.sum(jnp.exp(column_score - piece_max[None, :]), axis=0)
        column_max, column_sum = combine(column_max, column_sum, piece_max, piece_sum)
        return (column_max, column_sum), (row_max, row_sum)

    pieces = (source_pos.reshape(source_pos.shape[0], count, block_rows).transpose(1, 0, 2), source_pot.reshape(count, block_rows), source_logw.reshape(count, block_rows))
    start = (jnp.full((width,), lowest, jnp.float32), jnp.zeros((width,), jnp.float32))
    (column_max, column_sum), (row_max, row_sum) = lax.scan(one_piece, start, pieces)
    return row_max.reshape(rows), row_sum.reshape(rows), column_max, column_sum


def reference(x_pos, y_pos, f_pot, g_pot, x_logw, y_logw):
    blocks = N_BLK
    width = PT_DEV * N_GRP
    source_pos = x_pos.reshape(DIM, blocks, width).transpose(1, 0, 2)
    target_pos = y_pos.reshape(DIM, blocks, width).transpose(1, 0, 2)
    source_pot = f_pot.reshape(blocks, width)
    target_pot = g_pot.reshape(blocks, width)
    source_logw = x_logw.reshape(blocks, width)
    target_logw = y_logw.reshape(blocks, width)
    half = STEPS // 2
    offsets = jnp.arange(-half, half, dtype=jnp.int32)

    def per_source(carry, index):
        sources = (source_pos[index], source_pot[index], source_logw[index])

        def per_offset(inner, offset):
            row_max, row_sum, column_max, column_sum = inner
            target = (index + offset) % blocks
            targets = (target_pos[target], target_pot[target], target_logw[target])
            tile_max, tile_sum, part_max, part_sum = tile_terms(sources, targets)
            row_max, row_sum = combine(row_max, row_sum, tile_max, tile_sum)
            new_max, new_sum = combine(column_max[target], column_sum[target], part_max, part_sum)
            column_max = column_max.at[target].set(new_max)
            column_sum = column_sum.at[target].set(new_sum)
            return (row_max, row_sum, column_max, column_sum), None

        start = (jnp.full((width,), lowest, jnp.float32), jnp.zeros((width,), jnp.float32), carry[0], carry[1])
        (row_max, row_sum, column_max, column_sum), _ = lax.scan(per_offset, start, offsets)
        return (column_max, column_sum), (row_max, row_sum)

    init = (jnp.full((blocks, width), lowest, jnp.float32), jnp.zeros((blocks, width), jnp.float32))
    (column_max, column_sum), (row_max, row_sum) = lax.scan(per_source, init, jnp.arange(blocks, dtype=jnp.int32))
    f_new = -epsilon * (row_max + jnp.log(row_sum)).reshape(-1)
    g_new = -epsilon * (column_max + jnp.log(column_sum)).reshape(-1)
    return 0.5 * (f_pot + f_new), 0.5 * (g_pot + g_new)
```

```python
import jax
import jax.numpy as jnp
from jax import lax
from jax.experimental import pallas as pl
from jax.experimental.pallas import tpu as pltpu
from jax.sharding import PartitionSpec as P

TILES = 6
ROWS = 56
SLOTS = 16
DEPTH = 64
LOG2E = 1.4426950408889634
LN2 = 0.6931471805599453
SMALL = 2.0**-80
LARGE = 2.0**120
lowest = -1e30
MESH = pl.DeviceIdType.MESH


def split3(a):
    high = a.astype(jnp.bfloat16).astype(jnp.float32)
    rest = a - high
    mid = rest.astype(jnp.bfloat16).astype(jnp.float32)
    return high, mid, rest - mid


def lines(values):
    shape = (8, values[0].shape[1])
    row = lax.broadcasted_iota(jnp.int32, shape, 0)
    out = jnp.zeros(shape, jnp.float32)
    for k, value in enumerate(values):
        out = jnp.where(row == k, value, out)
    return out


def other_terms(pos, bias):
    high, mid, low = split3(pos)
    one = jnp.ones_like(bias)
    last = lines([*split3(bias), one, one, one])
    return jnp.concatenate([high, high, high, mid, mid, low, last, jnp.zeros_like(pos)], axis=0)


def own_terms(pos, bias):
    high, mid, low = split3(pos * LOG2E)
    one = jnp.ones_like(bias)
    last = lines([one, one, one, *split3(bias)])
    return jnp.concatenate([high, mid, low, high, mid, high, last, jnp.zeros_like(pos)], axis=0)


def pack_shard(pos_ref, pot_ref, logw_ref, out_ref):
    for j in range(TILES):
        pos = pos_ref[:, 128 * j : 128 * j + 128]
        out_ref[8 * j : 8 * j + 8, :] = pos
        half = 0.5 * jnp.sum(pos * pos, axis=0, keepdims=True)
        bias = (logw_ref[j : j + 1, :] + pot_ref[j : j + 1, :] - half) * LOG2E
        out_ref[48 + j : 49 + j, :] = bias
    out_ref[54:56, :] = jnp.zeros((2, 128), jnp.float32)


def peer(zone, e, d, outward):
    block = lax.axis_index("blk")
    place = block % 4
    core, high = place % 2, place // 2
    other = (core + e) % 2 + 2 * ((high + e // 2) % 2)
    step = other - place
    if outward:
        up = (place - other + 4) // 4
        far = 8 * up - 4
    else:
        up = (other - place + 4) // 4
        far = 4 - 8 * up
    target = (block + step + zone * far + 64) % 64
    return (target, (lax.axis_index("grp") + d) % 2)


def at_step(n):
    zone = 1 - (n - 1) // 8
    w = zone * (n - 1) + (1 - zone) * (16 - n)
    near = (1 - zone) * (1 - (w + 5) // 8)
    w = w + near * (3 - 2 * w)
    return zone, w // 2, w % 2


def exchange_kernel(
    x_ref, y_ref, f_ref, g_ref, xl_ref, yl_ref,
    r_ref, c_ref, yh_ref, xh_ref,
    xs, ys, ybuf, lhs, rhs, racc, csend, cbuf,
    ysend, yrecv, xsend, xrecv, cs_sem, cr_sem, keep,
):
    barrier = pltpu.get_barrier_semaphore()
    greeted = [(zone, e, d, True) for zone in (0, 1) for e in range(4) for d in (0, 1)][1:]
    greeted += [(1, 0, d, False) for d in (0, 1)]
    for zone, e, d, outward in greeted:
        pl.semaphore_signal(barrier, inc=1, device_id=peer(zone, e, d, outward), device_id_type=MESH)

    pack_shard(y_ref, g_ref, yl_ref, ys)
    pack_shard(x_ref, f_ref, xl_ref, xs)
    csend[...] = jnp.zeros_like(csend)
    racc[...] = jnp.zeros_like(racc)
    for j in range(TILES):
        terms = own_terms(xs[8 * j : 8 * j + 8, :], xs[48 + j : 49 + j, :])
        lhs[128 * j : 128 * j + 128, :] = terms.T.astype(jnp.bfloat16)
    pl.semaphore_wait(barrier, len(greeted))

    def y_copy(zone, e, d, outward):
        slot = zone * 8 + e * 2 + d
        return pltpu.make_async_remote_copy(
            ys, ybuf.at[slot], ysend.at[slot], yrecv.at[slot],
            device_id=peer(zone, e, d, outward), device_id_type=MESH,
        )

    def x_copy(zone, e, d):
        slot = zone * 8 + e * 2 + d
        return pltpu.make_async_remote_copy(
            xs, xh_ref.at[slot], xsend.at[slot], xrecv.at[slot],
            device_id=peer(zone, e, d, False), device_id_type=MESH,
        )

    def c_copy(zone, e, d):
        slot = zone * 8 + e * 2 + d
        return pltpu.make_async_remote_copy(
            csend.at[slot], cbuf.at[slot], cs_sem.at[slot], cr_sem.at[slot],
            device_id=peer(zone, e, d, False), device_id_type=MESH,
        )

    for n in range(1, SLOTS):
        y_copy(*at_step(n), True).start()
    for n in range(1, SLOTS):
        x_copy(*at_step(n)).start()
    keep_x = pltpu.make_async_copy(xs, xh_ref.at[0], keep.at[0])
    keep_x.start()

    def tile(shard, slot):
        for j in range(TILES):
            terms = other_terms(shard[8 * j : 8 * j + 8, :], shard[48 + j : 49 + j, :])
            rhs[:, 128 * j : 128 * j + 128] = terms.astype(jnp.bfloat16)
        for c in range(3):
            weights = rhs[:, 256 * c : 256 * c + 256]
            column = jnp.zeros((8, 256), jnp.float32)
            for t in range(0, 768, 128):
                score = jnp.dot(lhs[t : t + 128, :], weights, preferred_element_type=jnp.float32)
                plan = jnp.exp2(score)
                column = column + jnp.sum(plan.reshape(16, 8, 256), axis=0)
                racc[t : t + 128, :] += plan[:, :128] + plan[:, 128:]
            total = jnp.sum(column, axis=0, keepdims=True)
            csend[slot, 2 * c : 2 * c + 1, :] = total[:, :128]
            csend[slot, 2 * c + 1 : 2 * c + 2, :] = total[:, 128:]

    tile(ys, 0)

    def step(n, carry):
        zone, e, d = at_step(n)
        slot = zone * 8 + e * 2 + d
        y_copy(zone, e, d, True).wait_recv()
        tile(ybuf.at[slot], slot)
        c_copy(zone, e, d).start()
        return carry

    lax.fori_loop(1, SLOTS, step, 0)

    keep_y = pltpu.make_async_copy(ybuf.at[pl.ds(1, SLOTS - 1)], yh_ref.at[pl.ds(1, SLOTS - 1)], keep.at[1])
    keep_own = pltpu.make_async_copy(ys, yh_ref.at[0], keep.at[2])
    keep_y.start()
    keep_own.start()
    for j in range(TILES):
        block = racc[128 * j : 128 * j + 128, :].T
        r_ref[j : j + 1, :] = jnp.sum(block, axis=0, keepdims=True)
    for n in range(1, SLOTS):
        copy = c_copy(*at_step(n))
        copy.wait_recv()
        copy.wait_send()
    total = csend[0, :, :]
    for slot in range(1, SLOTS):
        total = total + cbuf[slot, :, :]
    c_ref[...] = total[:TILES, :]
    for n in range(1, SLOTS):
        y_copy(*at_step(n), True).wait_send()
        copy = x_copy(*at_step(n))
        copy.wait_send()
        copy.wait_recv()
    keep_x.wait()
    keep_y.wait()
    keep_own.wait()


def stable(own_pos_ref, others_hbm, shards, sem, lhs, rhs, top, acc, rows):
    copy = pltpu.make_async_copy(others_hbm, shards, sem)
    copy.start()
    for j in range(TILES):
        pos = own_pos_ref[:, 128 * j : 128 * j + 128]
        terms = own_terms(pos, jnp.zeros((1, 128), jnp.float32))
        rhs[:, 128 * j : 128 * j + 128] = terms.astype(jnp.bfloat16)
    top[...] = jnp.full_like(top, lowest)
    acc[...] = jnp.zeros_like(acc)
    copy.wait()

    def one(slot, carry):
        for j in range(TILES):
            terms = other_terms(shards[slot, 8 * j : 8 * j + 8, :], shards[slot, pl.ds(48 + j, 1), :])
            lhs[128 * j : 128 * j + 128, :] = terms.T.astype(jnp.bfloat16)
        for c in range(3):
            weights = rhs[:, 256 * c : 256 * c + 256]
            best, total = top[:, 256 * c : 256 * c + 256], acc[:, 256 * c : 256 * c + 256]
            for t in range(0, 768, 128):
                score = jnp.dot(lhs[t : t + 128, :], weights, preferred_element_type=jnp.float32)
                score = score.reshape(16, 8, 256)
                new = jnp.maximum(best, jnp.max(score, axis=0))
                total = total * jnp.exp2(best - new) + jnp.sum(jnp.exp2(score - new[None]), axis=0)
                best = new
            top[:, 256 * c : 256 * c + 256] = best
            acc[:, 256 * c : 256 * c + 256] = total
        return carry

    lax.fori_loop(0, SLOTS, one, 0)
    best = jnp.max(top[...], axis=0, keepdims=True)
    total = jnp.sum(acc[...] * jnp.exp2(top[...] - best), axis=0, keepdims=True)
    result = LN2 * (best + jnp.log2(total))
    for j in range(TILES):
        pos = own_pos_ref[:, 128 * j : 128 * j + 128]
        half = 0.5 * jnp.sum(pos * pos, axis=0, keepdims=True)
        rows[j : j + 1, :] = half - result[:, 128 * j : 128 * j + 128]


def finish_kernel(
    r_ref, c_ref, f_ref, g_ref, xl_ref, yl_ref, x_ref, y_ref, yh_ref, xh_ref,
    fo_ref, go_ref,
    own, shards, lhs, rhs, top, acc, rows, sem,
):
    f, g = f_ref[...], g_ref[...]
    r, c = r_ref[...], c_ref[...]
    fo_ref[...] = f + 0.5 * (xl_ref[...] - LN2 * jnp.log2(r))
    go_ref[...] = g + 0.5 * (yl_ref[...] - LN2 * jnp.log2(c))
    least = jnp.min(jnp.minimum(r, c))
    most = jnp.max(jnp.maximum(r, c))

    @pl.when(jnp.logical_not(jnp.logical_and(least >= SMALL, most <= LARGE)))
    def _():
        for pos_hbm, others_hbm, pot, out in ((x_ref, yh_ref, f, fo_ref), (y_ref, xh_ref, g, go_ref)):
            copy = pltpu.make_async_copy(pos_hbm, own, sem.at[0])
            copy.start()
            copy.wait()
            stable(own, others_hbm, shards, sem.at[1], lhs, rhs, top, acc, rows)
            out[...] = 0.5 * (pot + rows[...])


def shards(x_pos, y_pos, f_pot, g_pot, x_logw, y_logw):
    f, g, xl, yl = (a.reshape(TILES, 128) for a in (f_pot, g_pot, x_logw, y_logw))
    small = jax.ShapeDtypeStruct((TILES, 128), jnp.float32)
    gathered = jax.ShapeDtypeStruct((SLOTS, ROWS, 128), jnp.float32)
    vmem = pl.BlockSpec(memory_space=pltpu.VMEM)
    anywhere = pl.BlockSpec(memory_space=pl.ANY)
    f32, bf16 = jnp.float32, jnp.bfloat16
    r, c, yh, xh = pl.pallas_call(
        exchange_kernel,
        out_shape=(small, small, gathered, gathered),
        in_specs=[vmem] * 6,
        out_specs=(vmem, vmem, anywhere, anywhere),
        scratch_shapes=[
            pltpu.VMEM((ROWS, 128), f32),
            pltpu.VMEM((ROWS, 128), f32),
            pltpu.VMEM((SLOTS, ROWS, 128), f32),
            pltpu.VMEM((768, DEPTH), bf16),
            pltpu.VMEM((DEPTH, 768), bf16),
            pltpu.VMEM((768, 128), f32),
            pltpu.VMEM((SLOTS, 8, 128), f32),
            pltpu.VMEM((SLOTS, 8, 128), f32),
        ]
        + [pltpu.SemaphoreType.DMA((SLOTS,))] * 6
        + [pltpu.SemaphoreType.DMA((3,))],
        compiler_params=pltpu.CompilerParams(collective_id=0, has_side_effects=True),
        name="exchange",
    )(x_pos, y_pos, f, g, xl, yl)
    fo, go = pl.pallas_call(
        finish_kernel,
        out_shape=(small, small),
        in_specs=[vmem] * 6 + [anywhere] * 4,
        out_specs=(vmem, vmem),
        scratch_shapes=[
            pltpu.VMEM((8, 768), f32),
            pltpu.VMEM((SLOTS, ROWS, 128), f32),
            pltpu.VMEM((768, DEPTH), bf16),
            pltpu.VMEM((DEPTH, 768), bf16),
            pltpu.VMEM((8, 768), f32),
            pltpu.VMEM((8, 768), f32),
            pltpu.VMEM((TILES, 128), f32),
            pltpu.SemaphoreType.DMA((2,)),
        ],
        name="finish",
    )(r, c, f, g, xl, yl, x_pos, y_pos, yh, xh)
    return fo.reshape(-1), go.reshape(-1)


def solution(mesh):
    both = ("blk", "grp")
    return jax.shard_map(
        shards,
        mesh=mesh,
        in_specs=(P(None, both), P(None, both), P(both), P(both), P(both), P(both)),
        out_specs=(P(both), P(both)),
        check_vma=False,
    )
```

```python
import jax
import jax.numpy as jnp
from jax import lax
from jax.experimental import pallas as pl
from jax.experimental.pallas import tpu as pltpu
from jax.sharding import PartitionSpec as P

TILES = 6
ROWS = 56
SLOTS = 16
DEPTH = 64
LOG2E = 1.4426950408889634
LN2 = 0.6931471805599453
SMALL = 2.0**-80
LARGE = 2.0**120
lowest = -1e30
SLOT_PEERS = (
    (0, 0, 0), (0, 1, 0), (0, 0, 1), (0, 2, 1), (1, 0, 0), (1, 1, 0), (0, 1, 1), (0, 3, 1),
    (0, 2, 0), (0, 3, 0), (1, 0, 1), (1, 1, 1), (1, 2, 1), (1, 2, 0), (1, 3, 1), (1, 3, 0),
)
RELAY = {2: 6, 3: 7, 8: 9, 12: 14, 13: 15}
DIRECT = tuple(slot for slot in range(1, 16) if slot not in RELAY.values())
SHARED = 12
GROUPS = ((1,), (2, 3), (4, 5), (6, 7), (8, 9), (10, 11), (12,), (13,), (14,), (15,))
PASS_ON = {1: (2, 3), 3: (8,), 5: (12,), 6: (13,)}
NEAR_AFTER, NEAR_PASS_AFTER = (2, 5)
MESH = pl.DeviceIdType.MESH


def split3(a):
    high = a.astype(jnp.bfloat16).astype(jnp.float32)
    rest = a - high
    mid = rest.astype(jnp.bfloat16).astype(jnp.float32)
    return high, mid, rest - mid


def lines(values):
    shape = (8, values[0].shape[1])
    row = lax.broadcasted_iota(jnp.int32, shape, 0)
    out = jnp.zeros(shape, jnp.float32)
    for k, value in enumerate(values):
        out = jnp.where(row == k, value, out)
    return out


def other_terms(pos, bias):
    high, mid, low = split3(pos)
    one = jnp.ones_like(bias)
    last = lines([*split3(bias), one, one, one])
    return jnp.concatenate([high, high, high, mid, mid, low, last, jnp.zeros_like(pos)], axis=0)


def own_terms(pos, bias):
    high, mid, low = split3(pos * LOG2E)
    one = jnp.ones_like(bias)
    last = lines([one, one, one, *split3(bias)])
    return jnp.concatenate([high, mid, low, high, mid, high, last, jnp.zeros_like(pos)], axis=0)


def pack_shard(pos_ref, pot_ref, logw_ref, out_ref):
    for j in range(TILES):
        pos = pos_ref[:, 128 * j : 128 * j + 128]
        out_ref[8 * j : 8 * j + 8, :] = pos
        half = 0.5 * jnp.sum(pos * pos, axis=0, keepdims=True)
        bias = (logw_ref[j : j + 1, :] + pot_ref[j : j + 1, :] - half) * LOG2E
        out_ref[48 + j : 49 + j, :] = bias
    out_ref[54:56, :] = jnp.zeros((2, 128), jnp.float32)


def peer_table():
    block, line = lax.axis_index("blk"), lax.axis_index("grp")
    place = lax.rem(block, 4)
    core, high = lax.rem(place, 2), lax.div(place, 2)
    cores, highs = (core, 1 - core), (high, 1 - high)
    lines = (line, 1 - line)
    near, inward, outward = [], [], []
    for e in range(4):
        other = cores[e % 2] + 2 * highs[e // 2]
        base = block - place + other + 64
        near.append(block - place + other)
        inward.append(lax.rem(base + 4 - 8 * lax.div(other - place + 4, 4), 64))
        outward.append(lax.rem(base - 4 + 8 * lax.div(place - other + 4, 4), 64))

    def find(slot, out=False):
        zone, e, d = SLOT_PEERS[slot]
        return ((outward if out else inward)[e] if zone else near[e], lines[d])

    return find


def exchange_kernel(
    x_hbm, y_hbm, f_hbm, g_hbm, xl_hbm, yl_hbm,
    out_ref, yh_ref, xh_ref,
    xin, yin, fin, gin, xlin, ylin,
    xs, ys, ybuf, xbuf, xlhs, ylhs, rhs, racc, cacc, csend, cbuf,
    load, ysend, yrecv, xsend, xrecv, farsend, cs_sem, cr_sem, keep,
):
    find = peer_table()
    barrier = pltpu.get_barrier_semaphore()
    greeted = [find(slot) for slot in DIRECT] + [find(4, out=True), find(10, out=True)]
    for target in greeted:
        pl.semaphore_signal(barrier, inc=1, device_id=target, device_id_type=MESH)
    loads = [
        pltpu.make_async_copy(src, dst, load.at[k])
        for k, (src, dst) in enumerate(
            ((y_hbm, yin), (g_hbm, gin), (yl_hbm, ylin), (x_hbm, xin), (f_hbm, fin), (xl_hbm, xlin))
        )
    ]
    for copy in loads:
        copy.start()
    csend[...] = jnp.zeros_like(csend)
    racc[...] = jnp.zeros_like(racc)
    cacc[...] = jnp.zeros_like(cacc)
    for copy in loads:
        copy.wait()
    pack_shard(yin, gin, ylin, ys)
    pack_shard(xin, fin, xlin, xs)
    pl.semaphore_wait(barrier, len(greeted))

    def y_copy(slot, via=None):
        source = ys if via is None else ybuf.at[via]
        target = find(slot, out=True) if via is None else find(1)
        return pltpu.make_async_remote_copy(
            source, ybuf.at[slot], ysend, yrecv.at[slot], device_id=target, device_id_type=MESH
        )

    def x_copy(slot, via=None):
        target = find(slot) if via is None else find(1)
        if slot < SHARED:
            source = xs if via is None else xh_ref.at[via]
            return pltpu.make_async_remote_copy(
                source, xh_ref.at[slot], xsend, xrecv.at[slot], device_id=target, device_id_type=MESH
            )
        source = xs if via is None else xbuf.at[via - SHARED]
        return pltpu.make_async_remote_copy(
            source, xbuf.at[slot - SHARED], farsend, xrecv.at[slot], device_id=target, device_id_type=MESH
        )

    def c_copy(slot):
        return pltpu.make_async_remote_copy(
            csend.at[slot], cbuf.at[slot], cs_sem, cr_sem, device_id=find(slot), device_id_type=MESH
        )

    def all_of(ref, sem, start, size):
        part = ref.at[pl.ds(start, size)]
        return pltpu.make_async_copy(part, part, sem)

    for slot in DIRECT:
        y_copy(slot).start()
        if slot >= SHARED:
            x_copy(slot).start()
    pltpu.make_async_copy(xs, xh_ref.at[0], keep.at[0]).start()
    pltpu.make_async_copy(ys, yh_ref.at[0], keep.at[1]).start()
    for shard, lhs in ((xs, xlhs), (ys, ylhs)):
        for j in range(TILES):
            terms = own_terms(shard[8 * j : 8 * j + 8, :], shard[48 + j : 49 + j, :])
            lhs[128 * j : 128 * j + 128, :] = terms.T.astype(jnp.bfloat16)

    def prepare(shard, spot):
        for j in range(TILES):
            terms = other_terms(shard[8 * j : 8 * j + 8, :], shard[48 + j : 49 + j, :])
            rhs[spot, :, 128 * j : 128 * j + 128] = terms.astype(jnp.bfloat16)

    def shared_tile(spot, slot):
        for c in range(3):
            weights = rhs[spot, :, 256 * c : 256 * c + 256]
            column = jnp.zeros((8, 256), jnp.float32)
            for t in range(0, 768, 128):
                score = jnp.dot(xlhs[t : t + 128, :], weights, preferred_element_type=jnp.float32)
                plan = jnp.exp2(score)
                column = column + jnp.sum(plan.reshape(16, 8, 256), axis=0)
                racc[t : t + 128, :] += plan[:, :128] + plan[:, 128:]
            total = jnp.sum(column, axis=0, keepdims=True)
            csend[slot, 2 * c : 2 * c + 1, :] = total[:, :128]
            csend[slot, 2 * c + 1 : 2 * c + 2, :] = total[:, 128:]

    def row_tile(spot, lhs, acc):
        for c in range(3):
            weights = rhs[spot, :, 256 * c : 256 * c + 256]
            for t in range(0, 768, 128):
                score = jnp.dot(lhs[t : t + 128, :], weights, preferred_element_type=jnp.float32)
                plan = jnp.exp2(score)
                acc[t : t + 128, :] += plan[:, :128] + plan[:, 128:]

    prepare(ys, 0)
    shared_tile(0, 0)
    landed = set()

    def land(slot):
        if slot not in landed:
            landed.add(slot)
            y_copy(slot).wait_recv()
            if slot >= SHARED:
                x_copy(slot).wait_recv()

    for number, group in enumerate(GROUPS):
        for slot in PASS_ON.get(number, ()):
            land(slot)
            y_copy(RELAY[slot], via=slot).start()
            if slot >= SHARED:
                x_copy(RELAY[slot], via=slot).start()
        if number == NEAR_AFTER:
            for slot in DIRECT:
                if slot < SHARED:
                    x_copy(slot).start()
        if number == NEAR_PASS_AFTER:
            for slot, there in RELAY.items():
                if slot < SHARED:
                    x_copy(slot).wait_recv()
                    x_copy(there, via=slot).start()
        for slot in group:
            land(slot)
        for slot in group:
            pltpu.make_async_copy(ybuf.at[slot], yh_ref.at[slot], keep.at[2]).start()
            if slot >= SHARED:
                pltpu.make_async_copy(xbuf.at[slot - SHARED], xh_ref.at[slot], keep.at[3]).start()
        work = []
        for slot in group:
            work.append((ybuf.at[slot], slot, xlhs, racc))
            if slot >= SHARED:
                work.append((xbuf.at[slot - SHARED], slot, ylhs, cacc))
        for spot, (shard, slot, lhs, acc) in enumerate(work):
            prepare(shard, spot)
        for spot, (shard, slot, lhs, acc) in enumerate(work):
            if slot < SHARED:
                shared_tile(spot, slot)
            else:
                row_tile(spot, lhs, acc)
        for slot in group:
            if slot < SHARED:
                c_copy(slot).start()

    def over_lanes(acc):
        parts = [jnp.sum(acc[128 * j : 128 * j + 128, :].T, axis=0, keepdims=True) for j in range(TILES)]
        return jnp.concatenate(parts, axis=0)

    rows = over_lanes(racc)
    columns = over_lanes(cacc) if SHARED < SLOTS else jnp.zeros((TILES, 128), jnp.float32)
    f, g, xl, yl = fin[...], gin[...], xlin[...], ylin[...]
    out_ref[0:6, :] = f + 0.5 * (xl - LN2 * jnp.log2(rows))
    all_of(cbuf, cr_sem, 1, SHARED - 1).wait()
    total = csend[0, :, :]
    for slot in range(1, SHARED):
        total = total + cbuf[slot, :, :]
    columns = columns + total[:TILES, :]
    out_ref[8:14, :] = g + 0.5 * (yl - LN2 * jnp.log2(columns))
    out_ref[16:22, :] = jnp.minimum(rows, columns)
    out_ref[24:30, :] = jnp.maximum(rows, columns)
    all_of(csend, cs_sem, 1, SHARED - 1).wait()
    all_of(ybuf, ysend, 1, SLOTS - 1).wait()
    all_of(xh_ref, xsend, 1, SHARED - 1).wait()
    for slot in range(1, SHARED):
        if slot not in RELAY:
            x_copy(slot).wait_recv()
    pltpu.make_async_copy(xs, xh_ref.at[0], keep.at[0]).wait()
    pltpu.make_async_copy(ys, yh_ref.at[0], keep.at[1]).wait()
    all_of(yh_ref, keep.at[2], 1, SLOTS - 1).wait()
    if SHARED < SLOTS:
        all_of(xbuf, farsend, 0, SLOTS - SHARED).wait()
        all_of(xh_ref, keep.at[3], SHARED, SLOTS - SHARED).wait()


def stable(own_pos_ref, others_hbm, shards, sem, lhs, rhs, top, acc, rows):
    copy = pltpu.make_async_copy(others_hbm, shards, sem)
    copy.start()
    for j in range(TILES):
        pos = own_pos_ref[:, 128 * j : 128 * j + 128]
        terms = own_terms(pos, jnp.zeros((1, 128), jnp.float32))
        rhs[:, 128 * j : 128 * j + 128] = terms.astype(jnp.bfloat16)
    top[...] = jnp.full_like(top, lowest)
    acc[...] = jnp.zeros_like(acc)
    copy.wait()

    def one(slot, carry):
        for j in range(TILES):
            terms = other_terms(shards[slot, 8 * j : 8 * j + 8, :], shards[slot, pl.ds(48 + j, 1), :])
            lhs[128 * j : 128 * j + 128, :] = terms.T.astype(jnp.bfloat16)
        for c in range(3):
            weights = rhs[:, 256 * c : 256 * c + 256]
            best, total = top[:, 256 * c : 256 * c + 256], acc[:, 256 * c : 256 * c + 256]
            for t in range(0, 768, 128):
                score = jnp.dot(lhs[t : t + 128, :], weights, preferred_element_type=jnp.float32)
                score = score.reshape(16, 8, 256)
                new = jnp.maximum(best, jnp.max(score, axis=0))
                total = total * jnp.exp2(best - new) + jnp.sum(jnp.exp2(score - new[None]), axis=0)
                best = new
            top[:, 256 * c : 256 * c + 256] = best
            acc[:, 256 * c : 256 * c + 256] = total
        return carry

    lax.fori_loop(0, SLOTS, one, 0)
    best = jnp.max(top[...], axis=0, keepdims=True)
    total = jnp.sum(acc[...] * jnp.exp2(top[...] - best), axis=0, keepdims=True)
    result = LN2 * (best + jnp.log2(total))
    for j in range(TILES):
        pos = own_pos_ref[:, 128 * j : 128 * j + 128]
        half = 0.5 * jnp.sum(pos * pos, axis=0, keepdims=True)
        rows[j : j + 1, :] = half - result[:, 128 * j : 128 * j + 128]


def finish_kernel(
    sums_ref, x_ref, y_ref, f_ref, g_ref, yh_ref, xh_ref,
    fo_ref, go_ref,
    own, pot, shards, lhs, rhs, top, acc, rows, sem,
):
    fo_ref[...] = sums_ref[0:6, :]
    go_ref[...] = sums_ref[8:14, :]
    least = jnp.min(sums_ref[16:22, :])
    most = jnp.max(sums_ref[24:30, :])

    @pl.when(jnp.logical_not(jnp.logical_and(least >= SMALL, most <= LARGE)))
    def _():
        for pos_hbm, pot_hbm, others_hbm, out in ((x_ref, f_ref, yh_ref, fo_ref), (y_ref, g_ref, xh_ref, go_ref)):
            for src, dst in ((pos_hbm, own), (pot_hbm, pot)):
                copy = pltpu.make_async_copy(src, dst, sem.at[0])
                copy.start()
                copy.wait()
            stable(own, others_hbm, shards, sem.at[1], lhs, rhs, top, acc, rows)
            out[...] = 0.5 * (pot[...] + rows[...])


def shards(x_pos, y_pos, f_pot, g_pot, x_logw, y_logw):
    f, g, xl, yl = (a.reshape(TILES, 128) for a in (f_pot, g_pot, x_logw, y_logw))
    small = jax.ShapeDtypeStruct((TILES, 128), jnp.float32)
    gathered = jax.ShapeDtypeStruct((SLOTS, ROWS, 128), jnp.float32)
    vmem = pl.BlockSpec(memory_space=pltpu.VMEM)
    anywhere = pl.BlockSpec(memory_space=pl.ANY)
    f32, bf16 = jnp.float32, jnp.bfloat16
    sums, yh, xh = pl.pallas_call(
        exchange_kernel,
        out_shape=(jax.ShapeDtypeStruct((32, 128), f32), gathered, gathered),
        in_specs=[anywhere] * 6,
        out_specs=(vmem, anywhere, anywhere),
        scratch_shapes=[
            pltpu.VMEM((8, 768), f32),
            pltpu.VMEM((8, 768), f32),
            pltpu.VMEM((TILES, 128), f32),
            pltpu.VMEM((TILES, 128), f32),
            pltpu.VMEM((TILES, 128), f32),
            pltpu.VMEM((TILES, 128), f32),
            pltpu.VMEM((ROWS, 128), f32),
            pltpu.VMEM((ROWS, 128), f32),
            pltpu.VMEM((SLOTS, ROWS, 128), f32),
            pltpu.VMEM((max(SLOTS - SHARED, 1), ROWS, 128), f32),
            pltpu.VMEM((768, DEPTH), bf16),
            pltpu.VMEM((768, DEPTH), bf16),
            pltpu.VMEM((4, DEPTH, 768), bf16),
            pltpu.VMEM((768, 128), f32),
            pltpu.VMEM((768, 128), f32),
            pltpu.VMEM((SLOTS, 8, 128), f32),
            pltpu.VMEM((SLOTS, 8, 128), f32),
            pltpu.SemaphoreType.DMA((6,)),
            pltpu.SemaphoreType.DMA,
            pltpu.SemaphoreType.DMA((SLOTS,)),
            pltpu.SemaphoreType.DMA,
            pltpu.SemaphoreType.DMA((SLOTS,)),
            pltpu.SemaphoreType.DMA,
            pltpu.SemaphoreType.DMA,
            pltpu.SemaphoreType.DMA,
            pltpu.SemaphoreType.DMA((4,)),
        ],
        compiler_params=pltpu.CompilerParams(collective_id=0, has_side_effects=True),
        name="exchange",
    )(x_pos, y_pos, f, g, xl, yl)
    fo, go = pl.pallas_call(
        finish_kernel,
        out_shape=(small, small),
        in_specs=[vmem] + [anywhere] * 6,
        out_specs=(vmem, vmem),
        scratch_shapes=[
            pltpu.VMEM((8, 768), f32),
            pltpu.VMEM((TILES, 128), f32),
            pltpu.VMEM((SLOTS, ROWS, 128), f32),
            pltpu.VMEM((768, DEPTH), bf16),
            pltpu.VMEM((DEPTH, 768), bf16),
            pltpu.VMEM((8, 768), f32),
            pltpu.VMEM((8, 768), f32),
            pltpu.VMEM((TILES, 128), f32),
            pltpu.SemaphoreType.DMA((2,)),
        ],
        name="finish",
    )(sums, x_pos, y_pos, f, g, yh, xh)
    return fo.reshape(-1), go.reshape(-1)


def solution(mesh):
    both = ("blk", "grp")
    return jax.shard_map(
        shards,
        mesh=mesh,
        in_specs=(P(None, both), P(None, both), P(both), P(both), P(both), P(both)),
        out_specs=(P(both), P(both)),
        check_vma=False,
    )
```

```python
import jax
import jax.numpy as jnp
from jax import lax
from jax.experimental import pallas as pl
from jax.experimental.pallas import tpu as pltpu
from jax.sharding import PartitionSpec as P

TILES = 6
ROWS = 56
SLOTS = 16
DEPTH = 64
LOG2E = 1.4426950408889634
LN2 = 0.6931471805599453
SMALL = 2.0**-80
LARGE = 2.0**120
lowest = -1e30
SLOT_PEERS = (
    (0, 0, 0), (0, 1, 0), (0, 0, 1), (0, 2, 1), (1, 0, 0), (1, 1, 0), (0, 1, 1), (0, 3, 1),
    (0, 2, 0), (0, 3, 0), (1, 0, 1), (1, 1, 1), (1, 2, 1), (1, 2, 0), (1, 3, 1), (1, 3, 0),
)
RELAY = {2: 6, 3: 7, 8: 9, 12: 14, 13: 15}
DIRECT = tuple(slot for slot in range(1, 16) if slot not in RELAY.values())
SHARED = 12
GROUPS = ((1,), (2, 3), (4, 5), (6, 7), (8, 9), (10, 11), (12,), (13,), (14,), (15,))
PASS_ON = {1: (2, 3), 3: (8,), 5: (12,), 6: (13,)}
NEAR_AFTER, NEAR_PASS_AFTER, FAR_AFTER = (2, 5, 1)
MESH = pl.DeviceIdType.MESH


def split3(a):
    high = a.astype(jnp.bfloat16).astype(jnp.float32)
    rest = a - high
    mid = rest.astype(jnp.bfloat16).astype(jnp.float32)
    return high, mid, rest - mid


def lines(values):
    shape = (8, values[0].shape[1])
    row = lax.broadcasted_iota(jnp.int32, shape, 0)
    out = jnp.zeros(shape, jnp.float32)
    for k, value in enumerate(values):
        out = jnp.where(row == k, value, out)
    return out


def other_terms(pos, bias):
    high, mid, low = split3(pos)
    one = jnp.ones_like(bias)
    last = lines([*split3(bias), one, one, one])
    return jnp.concatenate([high, high, high, mid, mid, low, last, jnp.zeros_like(pos)], axis=0)


def own_terms(pos, bias):
    high, mid, low = split3(pos * LOG2E)
    one = jnp.ones_like(bias)
    last = lines([one, one, one, *split3(bias)])
    return jnp.concatenate([high, mid, low, high, mid, high, last, jnp.zeros_like(pos)], axis=0)


def pack_shard(pos_ref, pot_ref, logw_ref, out_ref):
    for j in range(TILES):
        pos = pos_ref[:, 128 * j : 128 * j + 128]
        out_ref[8 * j : 8 * j + 8, :] = pos
        half = 0.5 * jnp.sum(pos * pos, axis=0, keepdims=True)
        bias = (logw_ref[j : j + 1, :] + pot_ref[j : j + 1, :] - half) * LOG2E
        out_ref[48 + j : 49 + j, :] = bias
    out_ref[54:56, :] = jnp.zeros((2, 128), jnp.float32)


def peer_table():
    block, line = lax.axis_index("blk"), lax.axis_index("grp")
    place = lax.rem(block, 4)
    core, high = lax.rem(place, 2), lax.div(place, 2)
    cores, highs = (core, 1 - core), (high, 1 - high)
    lines = (line, 1 - line)
    near, inward, outward = [], [], []
    for e in range(4):
        other = cores[e % 2] + 2 * highs[e // 2]
        base = block - place + other + 64
        near.append(block - place + other)
        inward.append(lax.rem(base + 4 - 8 * lax.div(other - place + 4, 4), 64))
        outward.append(lax.rem(base - 4 + 8 * lax.div(place - other + 4, 4), 64))

    def find(slot, out=False):
        zone, e, d = SLOT_PEERS[slot]
        return ((outward if out else inward)[e] if zone else near[e], lines[d])

    return find


def exchange_kernel(
    x_hbm, y_hbm, f_hbm, g_hbm, xl_hbm, yl_hbm,
    out_ref, yh_ref, xh_ref,
    xin, yin, fin, gin, xlin, ylin,
    xs, ys, ybuf, xbuf, xlhs, ylhs, rhs, racc, cacc, csend, cbuf,
    load, ysend, yrecv, xsend, xrecv, farsend, cs_sem, cr_sem, keep, ready,
):
    find = peer_table()
    barrier = pltpu.get_barrier_semaphore()
    greeted = [find(slot) for slot in (3, 2, 4, 5, 1)] + [find(4, out=True)]
    for target in greeted:
        pl.semaphore_signal(barrier, inc=1, device_id=target, device_id_type=MESH)
    loads = [
        pltpu.make_async_copy(src, dst, load.at[k])
        for k, (src, dst) in enumerate(
            ((y_hbm, yin), (g_hbm, gin), (yl_hbm, ylin), (x_hbm, xin), (f_hbm, fin), (xl_hbm, xlin))
        )
    ]
    for copy in loads:
        copy.start()
    csend[...] = jnp.zeros_like(csend)
    racc[...] = jnp.zeros_like(racc)
    cacc[...] = jnp.zeros_like(cacc)
    for copy in loads:
        copy.wait()
    pack_shard(yin, gin, ylin, ys)
    pack_shard(xin, fin, xlin, xs)
    pl.semaphore_wait(barrier, len(greeted))

    def y_copy(slot, via=None):
        source = ys if via is None else ybuf.at[via]
        target = find(slot, out=True) if via is None else find(1)
        return pltpu.make_async_remote_copy(
            source, ybuf.at[slot], ysend, yrecv.at[slot], device_id=target, device_id_type=MESH
        )

    def x_copy(slot, via=None):
        target = find(slot) if via is None else find(1)
        if slot < SHARED:
            source = xs if via is None else xh_ref.at[via]
            return pltpu.make_async_remote_copy(
                source, xh_ref.at[slot], xsend, xrecv.at[slot], device_id=target, device_id_type=MESH
            )
        source = xs if via is None else xbuf.at[via - SHARED]
        return pltpu.make_async_remote_copy(
            source, xbuf.at[slot - SHARED], farsend, xrecv.at[slot], device_id=target, device_id_type=MESH
        )

    def c_copy(slot):
        return pltpu.make_async_remote_copy(
            csend.at[slot], cbuf.at[slot], cs_sem, cr_sem, device_id=find(slot), device_id_type=MESH
        )

    def all_of(ref, sem, start, size):
        part = ref.at[pl.ds(start, size)]
        return pltpu.make_async_copy(part, part, sem)

    def tell(slot, k):
        pl.semaphore_signal(ready.at[k], inc=1, device_id=find(slot), device_id_type=MESH)

    def send(slots):
        for slot in slots:
            y_copy(slot).start()
            if slot >= SHARED:
                x_copy(slot).start()

    for k, slot in ((0, 2), (1, 3)):
        tell(slot, k)
    send((2, 3, 4, 5, 1))

    def own_side(shard, lhs):
        for j in range(TILES):
            terms = own_terms(shard[8 * j : 8 * j + 8, :], shard[48 + j : 49 + j, :])
            lhs[128 * j : 128 * j + 128, :] = terms.T.astype(jnp.bfloat16)

    own_side(xs, xlhs)

    def prepare(shard, spot):
        for j in range(TILES):
            terms = other_terms(shard[8 * j : 8 * j + 8, :], shard[48 + j : 49 + j, :])
            rhs[spot, :, 128 * j : 128 * j + 128] = terms.astype(jnp.bfloat16)

    def shared_tile(spot, slot):
        for c in range(3):
            weights = rhs[spot, :, 256 * c : 256 * c + 256]
            column = jnp.zeros((8, 256), jnp.float32)
            for t in range(0, 768, 128):
                score = jnp.dot(xlhs[t : t + 128, :], weights, preferred_element_type=jnp.float32)
                plan = jnp.exp2(score)
                column = column + jnp.sum(plan.reshape(16, 8, 256), axis=0)
                racc[t : t + 128, :] += plan[:, :128] + plan[:, 128:]
            total = jnp.sum(column, axis=0, keepdims=True)
            csend[slot, 2 * c : 2 * c + 1, :] = total[:, :128]
            csend[slot, 2 * c + 1 : 2 * c + 2, :] = total[:, 128:]

    def row_tile(spot, lhs, acc):
        for c in range(3):
            weights = rhs[spot, :, 256 * c : 256 * c + 256]
            for t in range(0, 768, 128):
                score = jnp.dot(lhs[t : t + 128, :], weights, preferred_element_type=jnp.float32)
                plan = jnp.exp2(score)
                acc[t : t + 128, :] += plan[:, :128] + plan[:, 128:]

    prepare(ys, 0)
    shared_tile(0, 0)
    pl.semaphore_wait(ready.at[0], 1)
    tell(8, 2)
    send((8, 10, 11))
    pl.semaphore_wait(ready.at[1], 1)
    send((12,))
    pltpu.make_async_copy(xs, xh_ref.at[0], keep.at[0]).start()
    pltpu.make_async_copy(ys, yh_ref.at[0], keep.at[1]).start()
    own_side(ys, ylhs)
    landed = set()

    def land(slot):
        if slot not in landed:
            landed.add(slot)
            y_copy(slot).wait_recv()
            if slot >= SHARED:
                x_copy(slot).wait_recv()

    for number, group in enumerate(GROUPS):
        if number == FAR_AFTER:
            pl.semaphore_wait(ready.at[2], 1)
            send((13,))
        for slot in PASS_ON.get(number, ()):
            land(slot)
            y_copy(RELAY[slot], via=slot).start()
            if slot >= SHARED:
                x_copy(RELAY[slot], via=slot).start()
        if number == NEAR_AFTER:
            for slot in DIRECT:
                if slot < SHARED:
                    x_copy(slot).start()
        if number == NEAR_PASS_AFTER:
            for slot, there in RELAY.items():
                if slot < SHARED:
                    x_copy(slot).wait_recv()
                    x_copy(there, via=slot).start()
        for slot in group:
            land(slot)
        for slot in group:
            pltpu.make_async_copy(ybuf.at[slot], yh_ref.at[slot], keep.at[2]).start()
            if slot >= SHARED:
                pltpu.make_async_copy(xbuf.at[slot - SHARED], xh_ref.at[slot], keep.at[3]).start()
        work = []
        for slot in group:
            work.append((ybuf.at[slot], slot, xlhs, racc))
            if slot >= SHARED:
                work.append((xbuf.at[slot - SHARED], slot, ylhs, cacc))
        for spot, (shard, slot, lhs, acc) in enumerate(work):
            prepare(shard, spot)
        for spot, (shard, slot, lhs, acc) in enumerate(work):
            if slot < SHARED:
                shared_tile(spot, slot)
            else:
                row_tile(spot, lhs, acc)
        for slot in group:
            if slot < SHARED:
                c_copy(slot).start()

    def over_lanes(acc):
        parts = [jnp.sum(acc[128 * j : 128 * j + 128, :].T, axis=0, keepdims=True) for j in range(TILES)]
        return jnp.concatenate(parts, axis=0)

    rows = over_lanes(racc)
    columns = over_lanes(cacc) if SHARED < SLOTS else jnp.zeros((TILES, 128), jnp.float32)
    f, g, xl, yl = fin[...], gin[...], xlin[...], ylin[...]
    out_ref[0:6, :] = f + 0.5 * (xl - LN2 * jnp.log2(rows))
    all_of(cbuf, cr_sem, 1, SHARED - 1).wait()
    total = csend[0, :, :]
    for slot in range(1, SHARED):
        total = total + cbuf[slot, :, :]
    columns = columns + total[:TILES, :]
    out_ref[8:14, :] = g + 0.5 * (yl - LN2 * jnp.log2(columns))
    out_ref[16:22, :] = jnp.minimum(rows, columns)
    out_ref[24:30, :] = jnp.maximum(rows, columns)
    all_of(csend, cs_sem, 1, SHARED - 1).wait()
    all_of(ybuf, ysend, 1, SLOTS - 1).wait()
    all_of(xh_ref, xsend, 1, SHARED - 1).wait()
    for slot in range(1, SHARED):
        if slot not in RELAY:
            x_copy(slot).wait_recv()
    pltpu.make_async_copy(xs, xh_ref.at[0], keep.at[0]).wait()
    pltpu.make_async_copy(ys, yh_ref.at[0], keep.at[1]).wait()
    all_of(yh_ref, keep.at[2], 1, SLOTS - 1).wait()
    if SHARED < SLOTS:
        all_of(xbuf, farsend, 0, SLOTS - SHARED).wait()
        all_of(xh_ref, keep.at[3], SHARED, SLOTS - SHARED).wait()


def stable(own_pos_ref, others_hbm, shards, sem, lhs, rhs, top, acc, rows):
    copy = pltpu.make_async_copy(others_hbm, shards, sem)
    copy.start()
    for j in range(TILES):
        pos = own_pos_ref[:, 128 * j : 128 * j + 128]
        terms = own_terms(pos, jnp.zeros((1, 128), jnp.float32))
        rhs[:, 128 * j : 128 * j + 128] = terms.astype(jnp.bfloat16)
    top[...] = jnp.full_like(top, lowest)
    acc[...] = jnp.zeros_like(acc)
    copy.wait()

    def one(slot, carry):
        for j in range(TILES):
            terms = other_terms(shards[slot, 8 * j : 8 * j + 8, :], shards[slot, pl.ds(48 + j, 1), :])
            lhs[128 * j : 128 * j + 128, :] = terms.T.astype(jnp.bfloat16)
        for c in range(3):
            weights = rhs[:, 256 * c : 256 * c + 256]
            best, total = top[:, 256 * c : 256 * c + 256], acc[:, 256 * c : 256 * c + 256]
            for t in range(0, 768, 128):
                score = jnp.dot(lhs[t : t + 128, :], weights, preferred_element_type=jnp.float32)
                score = score.reshape(16, 8, 256)
                new = jnp.maximum(best, jnp.max(score, axis=0))
                total = total * jnp.exp2(best - new) + jnp.sum(jnp.exp2(score - new[None]), axis=0)
                best = new
            top[:, 256 * c : 256 * c + 256] = best
            acc[:, 256 * c : 256 * c + 256] = total
        return carry

    lax.fori_loop(0, SLOTS, one, 0)
    best = jnp.max(top[...], axis=0, keepdims=True)
    total = jnp.sum(acc[...] * jnp.exp2(top[...] - best), axis=0, keepdims=True)
    result = LN2 * (best + jnp.log2(total))
    for j in range(TILES):
        pos = own_pos_ref[:, 128 * j : 128 * j + 128]
        half = 0.5 * jnp.sum(pos * pos, axis=0, keepdims=True)
        rows[j : j + 1, :] = half - result[:, 128 * j : 128 * j + 128]


def finish_kernel(
    sums_ref, x_ref, y_ref, f_ref, g_ref, yh_ref, xh_ref,
    fo_ref, go_ref,
    own, pot, shards, lhs, rhs, top, acc, rows, sem,
):
    fo_ref[...] = sums_ref[0:6, :]
    go_ref[...] = sums_ref[8:14, :]
    least = jnp.min(sums_ref[16:22, :])
    most = jnp.max(sums_ref[24:30, :])

    @pl.when(jnp.logical_not(jnp.logical_and(least >= SMALL, most <= LARGE)))
    def _():
        for pos_hbm, pot_hbm, others_hbm, out in ((x_ref, f_ref, yh_ref, fo_ref), (y_ref, g_ref, xh_ref, go_ref)):
            for src, dst in ((pos_hbm, own), (pot_hbm, pot)):
                copy = pltpu.make_async_copy(src, dst, sem.at[0])
                copy.start()
                copy.wait()
            stable(own, others_hbm, shards, sem.at[1], lhs, rhs, top, acc, rows)
            out[...] = 0.5 * (pot[...] + rows[...])


def shards(x_pos, y_pos, f_pot, g_pot, x_logw, y_logw):
    f, g, xl, yl = (a.reshape(TILES, 128) for a in (f_pot, g_pot, x_logw, y_logw))
    small = jax.ShapeDtypeStruct((TILES, 128), jnp.float32)
    gathered = jax.ShapeDtypeStruct((SLOTS, ROWS, 128), jnp.float32)
    vmem = pl.BlockSpec(memory_space=pltpu.VMEM)
    anywhere = pl.BlockSpec(memory_space=pl.ANY)
    f32, bf16 = jnp.float32, jnp.bfloat16
    sums, yh, xh = pl.pallas_call(
        exchange_kernel,
        out_shape=(jax.ShapeDtypeStruct((32, 128), f32), gathered, gathered),
        in_specs=[anywhere] * 6,
        out_specs=(vmem, anywhere, anywhere),
        scratch_shapes=[
            pltpu.VMEM((8, 768), f32),
            pltpu.VMEM((8, 768), f32),
            pltpu.VMEM((TILES, 128), f32),
            pltpu.VMEM((TILES, 128), f32),
            pltpu.VMEM((TILES, 128), f32),
            pltpu.VMEM((TILES, 128), f32),
            pltpu.VMEM((ROWS, 128), f32),
            pltpu.VMEM((ROWS, 128), f32),
            pltpu.VMEM((SLOTS, ROWS, 128), f32),
            pltpu.VMEM((max(SLOTS - SHARED, 1), ROWS, 128), f32),
            pltpu.VMEM((768, DEPTH), bf16),
            pltpu.VMEM((768, DEPTH), bf16),
            pltpu.VMEM((4, DEPTH, 768), bf16),
            pltpu.VMEM((768, 128), f32),
            pltpu.VMEM((768, 128), f32),
            pltpu.VMEM((SLOTS, 8, 128), f32),
            pltpu.VMEM((SLOTS, 8, 128), f32),
            pltpu.SemaphoreType.DMA((6,)),
            pltpu.SemaphoreType.DMA,
            pltpu.SemaphoreType.DMA((SLOTS,)),
            pltpu.SemaphoreType.DMA,
            pltpu.SemaphoreType.DMA((SLOTS,)),
            pltpu.SemaphoreType.DMA,
            pltpu.SemaphoreType.DMA,
            pltpu.SemaphoreType.DMA,
            pltpu.SemaphoreType.DMA((4,)),
            pltpu.SemaphoreType.REGULAR((3,)),
        ],
        compiler_params=pltpu.CompilerParams(collective_id=0, has_side_effects=True),
        name="exchange",
    )(x_pos, y_pos, f, g, xl, yl)
    fo, go = pl.pallas_call(
        finish_kernel,
        out_shape=(small, small),
        in_specs=[vmem] + [anywhere] * 6,
        out_specs=(vmem, vmem),
        scratch_shapes=[
            pltpu.VMEM((8, 768), f32),
            pltpu.VMEM((TILES, 128), f32),
            pltpu.VMEM((SLOTS, ROWS, 128), f32),
            pltpu.VMEM((768, DEPTH), bf16),
            pltpu.VMEM((DEPTH, 768), bf16),
            pltpu.VMEM((8, 768), f32),
            pltpu.VMEM((8, 768), f32),
            pltpu.VMEM((TILES, 128), f32),
            pltpu.SemaphoreType.DMA((2,)),
        ],
        name="finish",
    )(sums, x_pos, y_pos, f, g, yh, xh)
    return fo.reshape(-1), go.reshape(-1)


def solution(mesh):
    both = ("blk", "grp")
    return jax.shard_map(
        shards,
        mesh=mesh,
        in_specs=(P(None, both), P(None, both), P(both), P(both), P(both), P(both)),
        out_specs=(P(both), P(both)),
        check_vma=False,
    )
```

```python
import jax
import jax.numpy as jnp
from jax import lax
from jax.experimental import pallas as pl
from jax.experimental.pallas import tpu as pltpu
from jax.sharding import PartitionSpec as P

TILES = 6
ROWS = 56
SLOTS = 16
DEPTH = 64
LOG2E = 1.4426950408889634
LN2 = 0.6931471805599453
SMALL = 2.0**-80
LARGE = 2.0**120
lowest = -1e30
SLOT_PEERS = (
    (0, 0, 0), (0, 1, 0), (0, 0, 1), (0, 2, 1), (1, 0, 0), (1, 1, 0), (0, 1, 1), (0, 3, 1),
    (0, 2, 0), (0, 3, 0), (1, 0, 1), (1, 1, 1), (1, 2, 1), (1, 2, 0), (1, 3, 1), (1, 3, 0),
)
RELAY = {2: 6, 3: 7, 8: 9, 12: 14, 13: 15}
DIRECT = tuple(slot for slot in range(1, 16) if slot not in RELAY.values())
SHARED = 12
GROUPS = ((1,), (2, 3), (6, 7), (8, 9), (4, 5), (10, 11), (12,), (13,), (14,), (15,))
PASS_ON = {1: (2, 3), 2: (8,), 5: (12,), 6: (13,)}
NEAR_AFTER, NEAR_PASS_AFTER, FAR_AFTER = (2, 5, 1)
MESH = pl.DeviceIdType.MESH


def split3(a):
    high = a.astype(jnp.bfloat16).astype(jnp.float32)
    rest = a - high
    mid = rest.astype(jnp.bfloat16).astype(jnp.float32)
    return high, mid, rest - mid


def lines(values):
    shape = (8, values[0].shape[1])
    row = lax.broadcasted_iota(jnp.int32, shape, 0)
    out = jnp.zeros(shape, jnp.float32)
    for k, value in enumerate(values):
        out = jnp.where(row == k, value, out)
    return out


def other_terms(pos, bias):
    high, mid, low = split3(pos)
    one = jnp.ones_like(bias)
    last = lines([*split3(bias), one, one, one])
    return jnp.concatenate([high, high, high, mid, mid, low, last, jnp.zeros_like(pos)], axis=0)


def own_terms(pos, bias):
    high, mid, low = split3(pos * LOG2E)
    one = jnp.ones_like(bias)
    last = lines([one, one, one, *split3(bias)])
    return jnp.concatenate([high, mid, low, high, mid, high, last, jnp.zeros_like(pos)], axis=0)


def pack_shard(pos_ref, pot_ref, logw_ref, out_ref):
    for j in range(TILES):
        pos = pos_ref[:, 128 * j : 128 * j + 128]
        out_ref[8 * j : 8 * j + 8, :] = pos
        half = 0.5 * jnp.sum(pos * pos, axis=0, keepdims=True)
        bias = (logw_ref[j : j + 1, :] + pot_ref[j : j + 1, :] - half) * LOG2E
        out_ref[48 + j : 49 + j, :] = bias
    out_ref[54:56, :] = jnp.zeros((2, 128), jnp.float32)


def peer_table():
    block, line = lax.axis_index("blk"), lax.axis_index("grp")
    place = lax.rem(block, 4)
    core, high = lax.rem(place, 2), lax.div(place, 2)
    cores, highs = (core, 1 - core), (high, 1 - high)
    lines = (line, 1 - line)
    near, inward, outward = [], [], []
    for e in range(4):
        other = cores[e % 2] + 2 * highs[e // 2]
        base = block - place + other + 64
        near.append(block - place + other)
        inward.append(lax.rem(base + 4 - 8 * lax.div(other - place + 4, 4), 64))
        outward.append(lax.rem(base - 4 + 8 * lax.div(place - other + 4, 4), 64))

    def find(slot, out=False):
        zone, e, d = SLOT_PEERS[slot]
        return ((outward if out else inward)[e] if zone else near[e], lines[d])

    return find


def exchange_kernel(
    x_hbm, y_hbm, f_hbm, g_hbm, xl_hbm, yl_hbm,
    out_ref, yh_ref, xh_ref,
    xin, yin, fin, gin, xlin, ylin,
    xs, ys, ybuf, xbuf, xlhs, ylhs, rhs, racc, cacc, csend, cbuf,
    load, ysend, yrecv, xsend, xrecv, farsend, cs_sem, cr_sem, keep, ready,
):
    find = peer_table()
    barrier = pltpu.get_barrier_semaphore()
    greeted = [find(slot) for slot in (8, 3, 2, 4, 5, 1)] + [find(4, out=True)]
    for target in greeted:
        pl.semaphore_signal(barrier, inc=1, device_id=target, device_id_type=MESH)
    loads = [
        pltpu.make_async_copy(src, dst, load.at[k])
        for k, (src, dst) in enumerate(
            ((y_hbm, yin), (g_hbm, gin), (yl_hbm, ylin), (x_hbm, xin), (f_hbm, fin), (xl_hbm, xlin))
        )
    ]
    for copy in loads:
        copy.start()
    csend[...] = jnp.zeros_like(csend)
    racc[...] = jnp.zeros_like(racc)
    cacc[...] = jnp.zeros_like(cacc)
    for copy in loads:
        copy.wait()
    pack_shard(yin, gin, ylin, ys)
    pack_shard(xin, fin, xlin, xs)
    pl.semaphore_wait(barrier, len(greeted))

    def y_copy(slot, via=None):
        source = ys if via is None else ybuf.at[via]
        target = find(slot, out=True) if via is None else find(1)
        return pltpu.make_async_remote_copy(
            source, ybuf.at[slot], ysend, yrecv.at[slot], device_id=target, device_id_type=MESH
        )

    def x_copy(slot, via=None):
        target = find(slot) if via is None else find(1)
        if slot < SHARED:
            source = xs if via is None else xh_ref.at[via]
            return pltpu.make_async_remote_copy(
                source, xh_ref.at[slot], xsend, xrecv.at[slot], device_id=target, device_id_type=MESH
            )
        source = xs if via is None else xbuf.at[via - SHARED]
        return pltpu.make_async_remote_copy(
            source, xbuf.at[slot - SHARED], farsend, xrecv.at[slot], device_id=target, device_id_type=MESH
        )

    def c_copy(slot):
        return pltpu.make_async_remote_copy(
            csend.at[slot], cbuf.at[slot], cs_sem, cr_sem, device_id=find(slot), device_id_type=MESH
        )

    def all_of(ref, sem, start, size):
        part = ref.at[pl.ds(start, size)]
        return pltpu.make_async_copy(part, part, sem)

    def tell(slot, k):
        pl.semaphore_signal(ready.at[k], inc=1, device_id=find(slot), device_id_type=MESH)

    def send(slots):
        for slot in slots:
            y_copy(slot).start()
            if slot >= SHARED:
                x_copy(slot).start()

    for k, slot in ((2, 8), (0, 2), (1, 3)):
        tell(slot, k)
    send((4, 5, 2, 3, 1, 8))

    def own_side(shard, lhs):
        for j in range(TILES):
            terms = own_terms(shard[8 * j : 8 * j + 8, :], shard[48 + j : 49 + j, :])
            lhs[128 * j : 128 * j + 128, :] = terms.T.astype(jnp.bfloat16)

    own_side(xs, xlhs)

    def prepare(shard, spot):
        for j in range(TILES):
            terms = other_terms(shard[8 * j : 8 * j + 8, :], shard[48 + j : 49 + j, :])
            rhs[spot, :, 128 * j : 128 * j + 128] = terms.astype(jnp.bfloat16)

    def shared_tile(spot, slot):
        for c in range(3):
            weights = rhs[spot, :, 256 * c : 256 * c + 256]
            column = jnp.zeros((8, 256), jnp.float32)
            for t in range(0, 768, 128):
                score = jnp.dot(xlhs[t : t + 128, :], weights, preferred_element_type=jnp.float32)
                plan = jnp.exp2(score)
                column = column + jnp.sum(plan.reshape(16, 8, 256), axis=0)
                racc[t : t + 128, :] += plan[:, :128] + plan[:, 128:]
            total = jnp.sum(column, axis=0, keepdims=True)
            csend[slot, 2 * c : 2 * c + 1, :] = total[:, :128]
            csend[slot, 2 * c + 1 : 2 * c + 2, :] = total[:, 128:]

    def row_tile(spot, lhs, acc):
        for c in range(3):
            weights = rhs[spot, :, 256 * c : 256 * c + 256]
            for t in range(0, 768, 128):
                score = jnp.dot(lhs[t : t + 128, :], weights, preferred_element_type=jnp.float32)
                plan = jnp.exp2(score)
                acc[t : t + 128, :] += plan[:, :128] + plan[:, 128:]

    prepare(ys, 0)
    shared_tile(0, 0)
    pl.semaphore_wait(ready.at[0], 1)
    send((10, 11))
    pl.semaphore_wait(ready.at[1], 1)
    send((12,))
    pltpu.make_async_copy(xs, xh_ref.at[0], keep.at[0]).start()
    pltpu.make_async_copy(ys, yh_ref.at[0], keep.at[1]).start()
    own_side(ys, ylhs)
    landed = set()

    def land(slot):
        if slot not in landed:
            landed.add(slot)
            y_copy(slot).wait_recv()
            if slot >= SHARED:
                x_copy(slot).wait_recv()

    for number, group in enumerate(GROUPS):
        if number == FAR_AFTER:
            pl.semaphore_wait(ready.at[2], 1)
            send((13,))
        for slot in PASS_ON.get(number, ()):
            land(slot)
            y_copy(RELAY[slot], via=slot).start()
            if slot >= SHARED:
                x_copy(RELAY[slot], via=slot).start()
        if number == NEAR_AFTER:
            for slot in DIRECT:
                if slot < SHARED:
                    x_copy(slot).start()
        if number == NEAR_PASS_AFTER:
            for slot, there in RELAY.items():
                if slot < SHARED:
                    x_copy(slot).wait_recv()
                    x_copy(there, via=slot).start()
        for slot in group:
            land(slot)
        for slot in group:
            pltpu.make_async_copy(ybuf.at[slot], yh_ref.at[slot], keep.at[2]).start()
            if slot >= SHARED:
                pltpu.make_async_copy(xbuf.at[slot - SHARED], xh_ref.at[slot], keep.at[3]).start()
        work = []
        for slot in group:
            work.append((ybuf.at[slot], slot, xlhs, racc))
            if slot >= SHARED:
                work.append((xbuf.at[slot - SHARED], slot, ylhs, cacc))
        for spot, (shard, slot, lhs, acc) in enumerate(work):
            prepare(shard, spot)
        for spot, (shard, slot, lhs, acc) in enumerate(work):
            if slot < SHARED:
                shared_tile(spot, slot)
            else:
                row_tile(spot, lhs, acc)
        for slot in group:
            if slot < SHARED:
                c_copy(slot).start()

    def over_lanes(acc):
        parts = [jnp.sum(acc[128 * j : 128 * j + 128, :].T, axis=0, keepdims=True) for j in range(TILES)]
        return jnp.concatenate(parts, axis=0)

    rows = over_lanes(racc)
    columns = over_lanes(cacc) if SHARED < SLOTS else jnp.zeros((TILES, 128), jnp.float32)
    f, g, xl, yl = fin[...], gin[...], xlin[...], ylin[...]
    out_ref[0:6, :] = f + 0.5 * (xl - LN2 * jnp.log2(rows))
    all_of(cbuf, cr_sem, 1, SHARED - 1).wait()
    total = csend[0, :, :]
    for slot in range(1, SHARED):
        total = total + cbuf[slot, :, :]
    columns = columns + total[:TILES, :]
    out_ref[8:14, :] = g + 0.5 * (yl - LN2 * jnp.log2(columns))
    out_ref[16:22, :] = jnp.minimum(rows, columns)
    out_ref[24:30, :] = jnp.maximum(rows, columns)
    all_of(csend, cs_sem, 1, SHARED - 1).wait()
    all_of(ybuf, ysend, 1, SLOTS - 1).wait()
    all_of(xh_ref, xsend, 1, SHARED - 1).wait()
    for slot in range(1, SHARED):
        if slot not in RELAY:
            x_copy(slot).wait_recv()
    pltpu.make_async_copy(xs, xh_ref.at[0], keep.at[0]).wait()
    pltpu.make_async_copy(ys, yh_ref.at[0], keep.at[1]).wait()
    all_of(yh_ref, keep.at[2], 1, SLOTS - 1).wait()
    if SHARED < SLOTS:
        all_of(xbuf, farsend, 0, SLOTS - SHARED).wait()
        all_of(xh_ref, keep.at[3], SHARED, SLOTS - SHARED).wait()


def stable(own_pos_ref, others_hbm, shards, sem, lhs, rhs, top, acc, rows):
    copy = pltpu.make_async_copy(others_hbm, shards, sem)
    copy.start()
    for j in range(TILES):
        pos = own_pos_ref[:, 128 * j : 128 * j + 128]
        terms = own_terms(pos, jnp.zeros((1, 128), jnp.float32))
        rhs[:, 128 * j : 128 * j + 128] = terms.astype(jnp.bfloat16)
    top[...] = jnp.full_like(top, lowest)
    acc[...] = jnp.zeros_like(acc)
    copy.wait()

    def one(slot, carry):
        for j in range(TILES):
            terms = other_terms(shards[slot, 8 * j : 8 * j + 8, :], shards[slot, pl.ds(48 + j, 1), :])
            lhs[128 * j : 128 * j + 128, :] = terms.T.astype(jnp.bfloat16)
        for c in range(3):
            weights = rhs[:, 256 * c : 256 * c + 256]
            best, total = top[:, 256 * c : 256 * c + 256], acc[:, 256 * c : 256 * c + 256]
            for t in range(0, 768, 128):
                score = jnp.dot(lhs[t : t + 128, :], weights, preferred_element_type=jnp.float32)
                score = score.reshape(16, 8, 256)
                new = jnp.maximum(best, jnp.max(score, axis=0))
                total = total * jnp.exp2(best - new) + jnp.sum(jnp.exp2(score - new[None]), axis=0)
                best = new
            top[:, 256 * c : 256 * c + 256] = best
            acc[:, 256 * c : 256 * c + 256] = total
        return carry

    lax.fori_loop(0, SLOTS, one, 0)
    best = jnp.max(top[...], axis=0, keepdims=True)
    total = jnp.sum(acc[...] * jnp.exp2(top[...] - best), axis=0, keepdims=True)
    result = LN2 * (best + jnp.log2(total))
    for j in range(TILES):
        pos = own_pos_ref[:, 128 * j : 128 * j + 128]
        half = 0.5 * jnp.sum(pos * pos, axis=0, keepdims=True)
        rows[j : j + 1, :] = half - result[:, 128 * j : 128 * j + 128]


def finish_kernel(
    sums_ref, x_ref, y_ref, f_ref, g_ref, yh_ref, xh_ref,
    fo_ref, go_ref,
    own, pot, shards, lhs, rhs, top, acc, rows, sem,
):
    fo_ref[...] = sums_ref[0:6, :]
    go_ref[...] = sums_ref[8:14, :]
    least = jnp.min(sums_ref[16:22, :])
    most = jnp.max(sums_ref[24:30, :])

    @pl.when(jnp.logical_not(jnp.logical_and(least >= SMALL, most <= LARGE)))
    def _():
        for pos_hbm, pot_hbm, others_hbm, out in ((x_ref, f_ref, yh_ref, fo_ref), (y_ref, g_ref, xh_ref, go_ref)):
            for src, dst in ((pos_hbm, own), (pot_hbm, pot)):
                copy = pltpu.make_async_copy(src, dst, sem.at[0])
                copy.start()
                copy.wait()
            stable(own, others_hbm, shards, sem.at[1], lhs, rhs, top, acc, rows)
            out[...] = 0.5 * (pot[...] + rows[...])


def shards(x_pos, y_pos, f_pot, g_pot, x_logw, y_logw):
    f, g, xl, yl = (a.reshape(TILES, 128) for a in (f_pot, g_pot, x_logw, y_logw))
    small = jax.ShapeDtypeStruct((TILES, 128), jnp.float32)
    gathered = jax.ShapeDtypeStruct((SLOTS, ROWS, 128), jnp.float32)
    vmem = pl.BlockSpec(memory_space=pltpu.VMEM)
    anywhere = pl.BlockSpec(memory_space=pl.ANY)
    f32, bf16 = jnp.float32, jnp.bfloat16
    sums, yh, xh = pl.pallas_call(
        exchange_kernel,
        out_shape=(pltpu.VMEM((32, 128), f32), gathered, gathered),
        in_specs=[anywhere] * 6,
        out_specs=(vmem, anywhere, anywhere),
        scratch_shapes=[
            pltpu.VMEM((8, 768), f32),
            pltpu.VMEM((8, 768), f32),
            pltpu.VMEM((TILES, 128), f32),
            pltpu.VMEM((TILES, 128), f32),
            pltpu.VMEM((TILES, 128), f32),
            pltpu.VMEM((TILES, 128), f32),
            pltpu.VMEM((ROWS, 128), f32),
            pltpu.VMEM((ROWS, 128), f32),
            pltpu.VMEM((SLOTS, ROWS, 128), f32),
            pltpu.VMEM((max(SLOTS - SHARED, 1), ROWS, 128), f32),
            pltpu.VMEM((768, DEPTH), bf16),
            pltpu.VMEM((768, DEPTH), bf16),
            pltpu.VMEM((4, DEPTH, 768), bf16),
            pltpu.VMEM((768, 128), f32),
            pltpu.VMEM((768, 128), f32),
            pltpu.VMEM((SLOTS, 8, 128), f32),
            pltpu.VMEM((SLOTS, 8, 128), f32),
            pltpu.SemaphoreType.DMA((6,)),
            pltpu.SemaphoreType.DMA,
            pltpu.SemaphoreType.DMA((SLOTS,)),
            pltpu.SemaphoreType.DMA,
            pltpu.SemaphoreType.DMA((SLOTS,)),
            pltpu.SemaphoreType.DMA,
            pltpu.SemaphoreType.DMA,
            pltpu.SemaphoreType.DMA,
            pltpu.SemaphoreType.DMA((4,)),
            pltpu.SemaphoreType.REGULAR((3,)),
        ],
        compiler_params=pltpu.CompilerParams(collective_id=0, has_side_effects=True),
        name="exchange",
    )(x_pos, y_pos, f, g, xl, yl)
    fo, go = pl.pallas_call(
        finish_kernel,
        out_shape=(small, small),
        in_specs=[vmem] + [anywhere] * 6,
        out_specs=(vmem, vmem),
        scratch_shapes=[
            pltpu.VMEM((8, 768), f32),
            pltpu.VMEM((TILES, 128), f32),
            pltpu.VMEM((SLOTS, ROWS, 128), f32),
            pltpu.VMEM((768, DEPTH), bf16),
            pltpu.VMEM((DEPTH, 768), bf16),
            pltpu.VMEM((8, 768), f32),
            pltpu.VMEM((8, 768), f32),
            pltpu.VMEM((TILES, 128), f32),
            pltpu.SemaphoreType.DMA((2,)),
        ],
        name="finish",
    )(pltpu.with_memory_space_constraint(sums, pltpu.VMEM), x_pos, y_pos, f, g, yh, xh)
    return fo.reshape(-1), go.reshape(-1)


def solution(mesh):
    both = ("blk", "grp")
    return jax.shard_map(
        shards,
        mesh=mesh,
        in_specs=(P(None, both), P(None, both), P(both), P(both), P(both), P(both)),
        out_specs=(P(both), P(both)),
        check_vma=False,
    )
```

```python
import jax
import jax.numpy as jnp
from jax import lax
from jax.experimental import pallas as pl
from jax.experimental.pallas import tpu as pltpu
from jax.sharding import PartitionSpec as P

TILES = 6
ROWS = 56
SLOTS = 16
DEPTH = 64
LOG2E = 1.4426950408889634
LN2 = 0.6931471805599453
SMALL = 2.0**-80
LARGE = 2.0**120
lowest = -1e30
SLOT_PEERS = (
    (0, 0, 0), (0, 1, 0), (0, 0, 1), (0, 2, 1), (1, 0, 0), (1, 1, 0), (0, 1, 1), (0, 3, 1),
    (0, 2, 0), (0, 3, 0), (1, 0, 1), (1, 1, 1), (1, 2, 1), (1, 2, 0), (1, 3, 1), (1, 3, 0),
)
RELAY = {2: 6, 3: 7, 8: 9, 12: 14, 13: 15}
DIRECT = tuple(slot for slot in range(1, 16) if slot not in RELAY.values())
SHARED = 12
GROUPS = ((1,), (2, 3), (6, 7), (8, 9), (4, 5), (10, 11), (12,), (13,), (14,), (15,))
PASS_ON = {1: (2, 3), 2: (8,), 5: (12,), 6: (13,)}
NEAR_AFTER, NEAR_PASS_AFTER, FAR_AFTER = (2, 6, 1)
MESH = pl.DeviceIdType.MESH


def split3(a):
    high = a.astype(jnp.bfloat16).astype(jnp.float32)
    rest = a - high
    mid = rest.astype(jnp.bfloat16).astype(jnp.float32)
    return high, mid, rest - mid


def lines(values):
    shape = (8, values[0].shape[1])
    row = lax.broadcasted_iota(jnp.int32, shape, 0)
    out = jnp.zeros(shape, jnp.float32)
    for k, value in enumerate(values):
        out = jnp.where(row == k, value, out)
    return out


def other_terms(pos, bias):
    high, mid, low = split3(pos)
    one = jnp.ones_like(bias)
    last = lines([*split3(bias), one, one, one])
    return jnp.concatenate([high, high, high, mid, mid, low, last, jnp.zeros_like(pos)], axis=0)


def own_terms(pos, bias):
    high, mid, low = split3(pos * LOG2E)
    one = jnp.ones_like(bias)
    last = lines([one, one, one, *split3(bias)])
    return jnp.concatenate([high, mid, low, high, mid, high, last, jnp.zeros_like(pos)], axis=0)


def pack_shard(pos_ref, pot_ref, logw_ref, out_ref):
    for j in range(TILES):
        pos = pos_ref[:, 128 * j : 128 * j + 128]
        out_ref[8 * j : 8 * j + 8, :] = pos
        half = 0.5 * jnp.sum(pos * pos, axis=0, keepdims=True)
        bias = (logw_ref[j : j + 1, :] + pot_ref[j : j + 1, :] - half) * LOG2E
        out_ref[48 + j : 49 + j, :] = bias
    out_ref[54:56, :] = jnp.zeros((2, 128), jnp.float32)


def peer_table():
    block, line = lax.axis_index("blk"), lax.axis_index("grp")
    place = lax.rem(block, 4)
    core, high = lax.rem(place, 2), lax.div(place, 2)
    cores, highs = (core, 1 - core), (high, 1 - high)
    lines = (line, 1 - line)
    near, inward, outward = [], [], []
    for e in range(4):
        other = cores[e % 2] + 2 * highs[e // 2]
        base = block - place + other + 64
        near.append(block - place + other)
        inward.append(lax.rem(base + 4 - 8 * lax.div(other - place + 4, 4), 64))
        outward.append(lax.rem(base - 4 + 8 * lax.div(place - other + 4, 4), 64))

    def find(slot, out=False):
        zone, e, d = SLOT_PEERS[slot]
        return ((outward if out else inward)[e] if zone else near[e], lines[d])

    return find


def exchange_kernel(
    x_hbm, y_hbm, f_hbm, g_hbm, xl_hbm, yl_hbm,
    out_ref, yh_ref, xh_ref,
    xin, yin, fin, gin, xlin, ylin,
    xs, ys, ybuf, xbuf, xlhs, ylhs, rhs, racc, cacc, csend, cbuf,
    load, ysend, yrecv, xsend, xrecv, farsend, cs_sem, cr_sem, keep, ready,
):
    find = peer_table()
    barrier = pltpu.get_barrier_semaphore()
    greeted = [find(slot) for slot in (8, 3, 2, 4, 5, 1)] + [find(4, out=True)]
    for target in greeted:
        pl.semaphore_signal(barrier, inc=1, device_id=target, device_id_type=MESH)
    loads = [
        pltpu.make_async_copy(src, dst, load.at[k])
        for k, (src, dst) in enumerate(
            ((y_hbm, yin), (g_hbm, gin), (yl_hbm, ylin), (x_hbm, xin), (f_hbm, fin), (xl_hbm, xlin))
        )
    ]
    for copy in loads:
        copy.start()
    csend[...] = jnp.zeros_like(csend)
    racc[...] = jnp.zeros_like(racc)
    cacc[...] = jnp.zeros_like(cacc)
    for copy in loads[:3]:
        copy.wait()
    pack_shard(yin, gin, ylin, ys)
    pl.semaphore_wait(barrier, len(greeted))

    def y_copy(slot, via=None):
        source = ys if via is None else ybuf.at[via]
        target = find(slot, out=True) if via is None else find(1)
        return pltpu.make_async_remote_copy(
            source, ybuf.at[slot], ysend, yrecv.at[slot], device_id=target, device_id_type=MESH
        )

    def x_copy(slot, via=None):
        target = find(slot) if via is None else find(1)
        if slot < SHARED:
            source = xs if via is None else xh_ref.at[via]
            return pltpu.make_async_remote_copy(
                source, xh_ref.at[slot], xsend, xrecv.at[slot], device_id=target, device_id_type=MESH
            )
        source = xs if via is None else xbuf.at[via - SHARED]
        return pltpu.make_async_remote_copy(
            source, xbuf.at[slot - SHARED], farsend, xrecv.at[slot], device_id=target, device_id_type=MESH
        )

    def c_copy(slot):
        return pltpu.make_async_remote_copy(
            csend.at[slot], cbuf.at[slot], cs_sem, cr_sem, device_id=find(slot), device_id_type=MESH
        )

    def all_of(ref, sem, start, size):
        part = ref.at[pl.ds(start, size)]
        return pltpu.make_async_copy(part, part, sem)

    def tell(slot, k):
        pl.semaphore_signal(ready.at[k], inc=1, device_id=find(slot), device_id_type=MESH)

    def send(slots):
        for slot in slots:
            y_copy(slot).start()
            if slot >= SHARED:
                x_copy(slot).start()

    for k, slot in ((2, 8), (0, 2), (1, 3)):
        tell(slot, k)
    send((4, 5, 2, 3, 1, 8))

    def own_side(shard, lhs):
        for j in range(TILES):
            terms = own_terms(shard[8 * j : 8 * j + 8, :], shard[48 + j : 49 + j, :])
            lhs[128 * j : 128 * j + 128, :] = terms.T.astype(jnp.bfloat16)

    for copy in loads[3:]:
        copy.wait()
    pack_shard(xin, fin, xlin, xs)
    own_side(xs, xlhs)

    def prepare(shard, spot):
        for j in range(TILES):
            terms = other_terms(shard[8 * j : 8 * j + 8, :], shard[48 + j : 49 + j, :])
            rhs[spot, :, 128 * j : 128 * j + 128] = terms.astype(jnp.bfloat16)

    def shared_tile(spot, slot):
        for c in range(3):
            weights = rhs[spot, :, 256 * c : 256 * c + 256]
            column = jnp.zeros((8, 256), jnp.float32)
            for t in range(0, 768, 128):
                score = jnp.dot(xlhs[t : t + 128, :], weights, preferred_element_type=jnp.float32)
                plan = jnp.exp2(score)
                column = column + jnp.sum(plan.reshape(16, 8, 256), axis=0)
                racc[t : t + 128, :] += plan[:, :128] + plan[:, 128:]
            total = jnp.sum(column, axis=0, keepdims=True)
            csend[slot, 2 * c : 2 * c + 1, :] = total[:, :128]
            csend[slot, 2 * c + 1 : 2 * c + 2, :] = total[:, 128:]

    def row_tile(spot, lhs, acc):
        for c in range(3):
            weights = rhs[spot, :, 256 * c : 256 * c + 256]
            for t in range(0, 768, 128):
                score = jnp.dot(lhs[t : t + 128, :], weights, preferred_element_type=jnp.float32)
                plan = jnp.exp2(score)
                acc[t : t + 128, :] += plan[:, :128] + plan[:, 128:]

    prepare(ys, 0)
    shared_tile(0, 0)
    pl.semaphore_wait(ready.at[0], 1)
    send((10, 11))
    pl.semaphore_wait(ready.at[1], 1)
    send((12,))
    pltpu.make_async_copy(xs, xh_ref.at[0], keep.at[0]).start()
    pltpu.make_async_copy(ys, yh_ref.at[0], keep.at[1]).start()
    own_side(ys, ylhs)
    landed = set()

    def land(slot):
        if slot not in landed:
            landed.add(slot)
            y_copy(slot).wait_recv()
            if slot >= SHARED:
                x_copy(slot).wait_recv()

    for number, group in enumerate(GROUPS):
        if number == FAR_AFTER:
            pl.semaphore_wait(ready.at[2], 1)
            send((13,))
        for slot in PASS_ON.get(number, ()):
            land(slot)
            y_copy(RELAY[slot], via=slot).start()
            if slot >= SHARED:
                x_copy(RELAY[slot], via=slot).start()
        if number == NEAR_AFTER:
            for slot in DIRECT:
                if slot < SHARED:
                    x_copy(slot).start()
        if number == NEAR_PASS_AFTER:
            for slot, there in RELAY.items():
                if slot < SHARED:
                    x_copy(slot).wait_recv()
                    x_copy(there, via=slot).start()
        for slot in group:
            land(slot)
        for slot in group:
            pltpu.make_async_copy(ybuf.at[slot], yh_ref.at[slot], keep.at[2]).start()
            if slot >= SHARED:
                pltpu.make_async_copy(xbuf.at[slot - SHARED], xh_ref.at[slot], keep.at[3]).start()
        work = []
        for slot in group:
            work.append((ybuf.at[slot], slot, xlhs, racc))
            if slot >= SHARED:
                work.append((xbuf.at[slot - SHARED], slot, ylhs, cacc))
        for spot, (shard, slot, lhs, acc) in enumerate(work):
            prepare(shard, spot)
        for spot, (shard, slot, lhs, acc) in enumerate(work):
            if slot < SHARED:
                shared_tile(spot, slot)
            else:
                row_tile(spot, lhs, acc)
        for slot in group:
            if slot < SHARED:
                c_copy(slot).start()

    def over_lanes(acc):
        parts = [jnp.sum(acc[128 * j : 128 * j + 128, :].T, axis=0, keepdims=True) for j in range(TILES)]
        return jnp.concatenate(parts, axis=0)

    rows = over_lanes(racc)
    columns = over_lanes(cacc) if SHARED < SLOTS else jnp.zeros((TILES, 128), jnp.float32)
    f, g, xl, yl = fin[...], gin[...], xlin[...], ylin[...]
    out_ref[0:6, :] = f + 0.5 * (xl - LN2 * jnp.log2(rows))
    all_of(cbuf, cr_sem, 1, SHARED - 1).wait()
    total = csend[0, :, :]
    for slot in range(1, SHARED):
        total = total + cbuf[slot, :, :]
    columns = columns + total[:TILES, :]
    out_ref[8:14, :] = g + 0.5 * (yl - LN2 * jnp.log2(columns))
    out_ref[16:22, :] = jnp.minimum(rows, columns)
    out_ref[24:30, :] = jnp.maximum(rows, columns)
    all_of(csend, cs_sem, 1, SHARED - 1).wait()
    all_of(ybuf, ysend, 1, SLOTS - 1).wait()
    all_of(xh_ref, xsend, 1, SHARED - 1).wait()
    for slot in range(1, SHARED):
        if slot not in RELAY:
            x_copy(slot).wait_recv()
    pltpu.make_async_copy(xs, xh_ref.at[0], keep.at[0]).wait()
    pltpu.make_async_copy(ys, yh_ref.at[0], keep.at[1]).wait()
    all_of(yh_ref, keep.at[2], 1, SLOTS - 1).wait()
    if SHARED < SLOTS:
        all_of(xbuf, farsend, 0, SLOTS - SHARED).wait()
        all_of(xh_ref, keep.at[3], SHARED, SLOTS - SHARED).wait()


def stable(own_pos_ref, others_hbm, shards, sem, lhs, rhs, top, acc, rows):
    copy = pltpu.make_async_copy(others_hbm, shards, sem)
    copy.start()
    for j in range(TILES):
        pos = own_pos_ref[:, 128 * j : 128 * j + 128]
        terms = own_terms(pos, jnp.zeros((1, 128), jnp.float32))
        rhs[:, 128 * j : 128 * j + 128] = terms.astype(jnp.bfloat16)
    top[...] = jnp.full_like(top, lowest)
    acc[...] = jnp.zeros_like(acc)
    copy.wait()

    def one(slot, carry):
        for j in range(TILES):
            terms = other_terms(shards[slot, 8 * j : 8 * j + 8, :], shards[slot, pl.ds(48 + j, 1), :])
            lhs[128 * j : 128 * j + 128, :] = terms.T.astype(jnp.bfloat16)
        for c in range(3):
            weights = rhs[:, 256 * c : 256 * c + 256]
            best, total = top[:, 256 * c : 256 * c + 256], acc[:, 256 * c : 256 * c + 256]
            for t in range(0, 768, 128):
                score = jnp.dot(lhs[t : t + 128, :], weights, preferred_element_type=jnp.float32)
                score = score.reshape(16, 8, 256)
                new = jnp.maximum(best, jnp.max(score, axis=0))
                total = total * jnp.exp2(best - new) + jnp.sum(jnp.exp2(score - new[None]), axis=0)
                best = new
            top[:, 256 * c : 256 * c + 256] = best
            acc[:, 256 * c : 256 * c + 256] = total
        return carry

    lax.fori_loop(0, SLOTS, one, 0)
    best = jnp.max(top[...], axis=0, keepdims=True)
    total = jnp.sum(acc[...] * jnp.exp2(top[...] - best), axis=0, keepdims=True)
    result = LN2 * (best + jnp.log2(total))
    for j in range(TILES):
        pos = own_pos_ref[:, 128 * j : 128 * j + 128]
        half = 0.5 * jnp.sum(pos * pos, axis=0, keepdims=True)
        rows[j : j + 1, :] = half - result[:, 128 * j : 128 * j + 128]


def finish_kernel(
    sums_ref, x_ref, y_ref, f_ref, g_ref, yh_ref, xh_ref,
    fo_ref, go_ref,
    own, pot, shards, lhs, rhs, top, acc, rows, sem,
):
    fo_ref[...] = sums_ref[0:6, :]
    go_ref[...] = sums_ref[8:14, :]
    least = jnp.min(sums_ref[16:22, :])
    most = jnp.max(sums_ref[24:30, :])

    @pl.when(jnp.logical_not(jnp.logical_and(least >= SMALL, most <= LARGE)))
    def _():
        for pos_hbm, pot_hbm, others_hbm, out in ((x_ref, f_ref, yh_ref, fo_ref), (y_ref, g_ref, xh_ref, go_ref)):
            for src, dst in ((pos_hbm, own), (pot_hbm, pot)):
                copy = pltpu.make_async_copy(src, dst, sem.at[0])
                copy.start()
                copy.wait()
            stable(own, others_hbm, shards, sem.at[1], lhs, rhs, top, acc, rows)
            out[...] = 0.5 * (pot[...] + rows[...])


def shards(x_pos, y_pos, f_pot, g_pot, x_logw, y_logw):
    f, g, xl, yl = (a.reshape(TILES, 128) for a in (f_pot, g_pot, x_logw, y_logw))
    small = jax.ShapeDtypeStruct((TILES, 128), jnp.float32)
    gathered = jax.ShapeDtypeStruct((SLOTS, ROWS, 128), jnp.float32)
    vmem = pl.BlockSpec(memory_space=pltpu.VMEM)
    anywhere = pl.BlockSpec(memory_space=pl.ANY)
    f32, bf16 = jnp.float32, jnp.bfloat16
    sums, yh, xh = pl.pallas_call(
        exchange_kernel,
        out_shape=(pltpu.VMEM((32, 128), f32), gathered, gathered),
        in_specs=[anywhere] * 6,
        out_specs=(vmem, anywhere, anywhere),
        scratch_shapes=[
            pltpu.VMEM((8, 768), f32),
            pltpu.VMEM((8, 768), f32),
            pltpu.VMEM((TILES, 128), f32),
            pltpu.VMEM((TILES, 128), f32),
            pltpu.VMEM((TILES, 128), f32),
            pltpu.VMEM((TILES, 128), f32),
            pltpu.VMEM((ROWS, 128), f32),
            pltpu.VMEM((ROWS, 128), f32),
            pltpu.VMEM((SLOTS, ROWS, 128), f32),
            pltpu.VMEM((max(SLOTS - SHARED, 1), ROWS, 128), f32),
            pltpu.VMEM((768, DEPTH), bf16),
            pltpu.VMEM((768, DEPTH), bf16),
            pltpu.VMEM((4, DEPTH, 768), bf16),
            pltpu.VMEM((768, 128), f32),
            pltpu.VMEM((768, 128), f32),
            pltpu.VMEM((SLOTS, 8, 128), f32),
            pltpu.VMEM((SLOTS, 8, 128), f32),
            pltpu.SemaphoreType.DMA((6,)),
            pltpu.SemaphoreType.DMA,
            pltpu.SemaphoreType.DMA((SLOTS,)),
            pltpu.SemaphoreType.DMA,
            pltpu.SemaphoreType.DMA((SLOTS,)),
            pltpu.SemaphoreType.DMA,
            pltpu.SemaphoreType.DMA,
            pltpu.SemaphoreType.DMA,
            pltpu.SemaphoreType.DMA((4,)),
            pltpu.SemaphoreType.REGULAR((3,)),
        ],
        compiler_params=pltpu.CompilerParams(collective_id=0, has_side_effects=True),
        name="exchange",
    )(x_pos, y_pos, f, g, xl, yl)
    fo, go = pl.pallas_call(
        finish_kernel,
        out_shape=(small, small),
        in_specs=[vmem] + [anywhere] * 6,
        out_specs=(vmem, vmem),
        scratch_shapes=[
            pltpu.VMEM((8, 768), f32),
            pltpu.VMEM((TILES, 128), f32),
            pltpu.VMEM((SLOTS, ROWS, 128), f32),
            pltpu.VMEM((768, DEPTH), bf16),
            pltpu.VMEM((DEPTH, 768), bf16),
            pltpu.VMEM((8, 768), f32),
            pltpu.VMEM((8, 768), f32),
            pltpu.VMEM((TILES, 128), f32),
            pltpu.SemaphoreType.DMA((2,)),
        ],
        name="finish",
    )(pltpu.with_memory_space_constraint(sums, pltpu.VMEM), x_pos, y_pos, f, g, yh, xh)
    return fo.reshape(-1), go.reshape(-1)


def solution(mesh):
    both = ("blk", "grp")
    return jax.shard_map(
        shards,
        mesh=mesh,
        in_specs=(P(None, both), P(None, both), P(both), P(both), P(both), P(both)),
        out_specs=(P(both), P(both)),
        check_vma=False,
    )
```
